256 devices in a mesh: blk: 32 (over y_lo, z, core), grp: 8 (over y_hi, x).
Axes of the slice: x: 4, y: 4 (y_hi: 2, y_lo: 2; y = y_hi * 2 + y_lo), z: 8, core: 2. Of those that a mesh axis runs over, the one named last changes fastest.
Arguments:
- matrix_sat: float32 [2048, 131072], P('grp', 'blk'), may hold values from -0.046875 to 0.046875
- matrix_ter: float32 [2048, 131072], P('grp', 'blk'), may hold values from -0.046875 to 0.046875
- probes: float32 [16, 131072], P(None, 'blk'), may hold values from -6 to 6
Outputs:
- row_part: float32 [2, 16, 2048], P(None, None, 'grp')
- column_part: float32 [2, 16, 131072], P(None, None, ('blk', 'grp'))
- trace_terms: float32 [2, 16], replicated
The draws below stay inside these ranges and needn't reach their ends.
All inputs are finite; a program needn't handle non-finite values.
Results may differ from the reference program's by a relative error of at most 0.000096.
Values sent between devices are 32-bit elements; how exact they have to be, the bound alone decides.
No kernel may reach another device: no remote copies, remote signals or barrier semaphores. Data moves between devices by JAX's collectives and lax.ppermute only.
A program may use at most 64 MiB of HBM per device.

```python
import jax
import jax.numpy as jnp
from jax import lax

PROBES = 16
ORDER = 131072
SLAB = 2048


def shard_levels(rng, extent, cuts, low, top_value):
    def one(dim, blocks):
        draws = jax.random.uniform(jax.random.fold_in(jax.random.fold_in(rng, 6), dim), (blocks,), jnp.float32, low / len(cuts), top_value / len(cuts))
        return jnp.repeat(jnp.exp(draws), extent[dim] // blocks).reshape((-1,) + (1,) * (len(extent) - dim - 1))

    factor_of = one(*cuts[0])
    for cut in cuts[1:]:
        factor_of = factor_of * one(*cut)
    return factor_of


def normal_values(key, shape, spread, bound, pieces=(), held_as=jnp.bfloat16):
    drawn = spread * jax.random.normal(key, shape, jnp.float32)
    if pieces:
        drawn = drawn * shard_levels(key, shape, pieces, -0.22, 0.18)
    return jnp.clip(drawn, -bound, bound).astype(held_as)


def setup_inputs(seed: int = 0) -> dict:
    splits = jax.random.split(jax.random.key(seed), 4)
    return {
        "matrix_sat": normal_values(splits[0], (SLAB, ORDER), ((SLAB * ORDER) ** -0.25), 0.046875, ((0, 8), (1, 32)), jnp.float32),
        "matrix_ter": normal_values(splits[1], (SLAB, ORDER), ((SLAB * ORDER) ** -0.25), 0.046875, ((0, 8), (1, 32)), jnp.float32),
        "probes": normal_values(splits[2], (PROBES, ORDER), 1.0, 6.0, ((1, 32),), jnp.float32),
    }


def one_matrix(matrix, probes):
    rows = jnp.arange(SLAB, dtype=jnp.int32)
    upper_mask = rows[None, :] >= rows[:, None]
    strict_mask = rows[None, :] > rows[:, None]
    head = matrix[:, :SLAB]
    tail = matrix[:, SLAB:]
    slab_probes = probes[:, :SLAB]
    hp = lax.Precision.HIGHEST
    direct = jnp.dot(slab_probes, jnp.where(upper_mask, head, 0.0).T, precision=hp)
    direct = direct + jnp.dot(probes[:, SLAB:], tail.T, precision=hp)
    mirror_head = jnp.dot(slab_probes, jnp.where(strict_mask, head, 0.0), precision=hp)
    mirror_tail = jnp.dot(slab_probes, tail, precision=hp)
    mirrored = jnp.concatenate([mirror_head, mirror_tail], axis=1)
    trace = jnp.sum(slab_probes * direct, axis=1) + jnp.sum(probes * mirrored, axis=1)
    return direct, mirrored, trace


def reference(matrix_sat, matrix_ter, probes):
    d_one, m_one, t_one = one_matrix(matrix_sat, probes)
    d_two, m_two, t_two = one_matrix(matrix_ter, probes)
    return jnp.stack([d_one, d_two]), jnp.stack([m_one, m_two]), jnp.stack([t_one, t_two])
```

```python
import functools

import jax
import jax.numpy as jnp
from jax import lax
from jax.experimental import pallas as pl
from jax.experimental.pallas import tpu as pltpu
from jax.sharding import Mesh
from jax.sharding import PartitionSpec as P

BLK = ("blk_0", "blk_1", "blk_2")
GRP = ("grp_0", "grp_1")
BLK_GRP = BLK + GRP
WIDTH = 1024
f32, bf16 = jnp.float32, jnp.bfloat16
VMEM = pl.BlockSpec(memory_space=pltpu.VMEM)


def halves(value):
    high = value.astype(bf16)
    return high, (value - high.astype(f32)).astype(bf16)


def stacked_halves(value):
    return jnp.concatenate(halves(value), axis=0)


def fold(both):
    half = both.shape[0] // 2
    return both[:half] + both[half:]


def dot_rows(probes_hl, matrix):
    high, low = halves(matrix)
    dims = (((1,), (1,)), ((), ()))
    return fold(
        lax.dot_general(probes_hl, high, dims, preferred_element_type=f32)
        + lax.dot_general(probes_hl, low, dims, preferred_element_type=f32)
    )


def dot_columns(slab_hl, matrix):
    high, low = halves(matrix)
    return fold(
        jnp.dot(slab_hl, high, preferred_element_type=f32)
        + jnp.dot(slab_hl, low, preferred_element_type=f32)
    )


def offsets(rows, cols):
    return lax.axis_index(GRP) * rows, lax.axis_index(BLK) * cols


def ids(shape, row0, col0):
    return (
        row0 + lax.broadcasted_iota(jnp.int32, shape, 0),
        col0 + lax.broadcasted_iota(jnp.int32, shape, 1),
    )


def row_kernel(cols, sat, ter, probes, out):
    step = pl.program_id(0)
    rows = sat.shape[0]
    n = probes.shape[0]
    row0, dev_col0 = offsets(rows, cols)
    col0 = dev_col0 + step * WIDTH

    @pl.when(step == 0)
    def _():
        out[...] = jnp.zeros_like(out)

    probes_hl = stacked_halves(probes[...])
    crossed = col0 < row0 + rows

    @pl.when(jnp.logical_not(crossed))
    def _():
        for k, matrix in enumerate((sat, ter)):
            out[k * n : (k + 1) * n] += dot_rows(probes_hl, matrix[...])

    @pl.when(crossed)
    def _():
        r, c = ids(sat.shape, row0, col0)
        for k, matrix in enumerate((sat, ter)):
            kept = jnp.where(c >= r, matrix[...], 0.0)
            out[k * n : (k + 1) * n] += dot_rows(probes_hl, kept)

    @pl.when((row0 >= col0) & (row0 < col0 + WIDTH))
    def _():
        at = pl.ds(pl.multiple_of(row0 - col0, rows), rows)
        out[2 * n : 3 * n] = probes[:, at]
        r, c = ids((rows, rows), 0, 0)
        for k, matrix in enumerate((sat, ter)):
            diagonal = jnp.sum(jnp.where(r == c, matrix[:, at], 0.0), axis=0, keepdims=True)
            out[3 * n + k : 3 * n + k + 1] = diagonal


def row_products(sat, ter, probes):
    rows, cols = sat.shape
    n = probes.shape[0]
    return pl.pallas_call(
        functools.partial(row_kernel, cols),
        grid=(cols // WIDTH,),
        in_specs=[
            pl.BlockSpec((rows, WIDTH), lambda j: (0, j)),
            pl.BlockSpec((rows, WIDTH), lambda j: (0, j)),
            pl.BlockSpec((n, WIDTH), lambda j: (0, j)),
        ],
        out_specs=pl.BlockSpec((3 * n + 8, rows), lambda j: (0, 0)),
        out_shape=jax.ShapeDtypeStruct((3 * n + 8, rows), f32),
        name="row_products",
    )(sat, ter, probes)


def column_kernel(cols, n, parts, sat, ter, shared, out, row_part):
    step = pl.program_id(0)
    rows = sat.shape[0]
    row0, dev_col0 = offsets(rows, cols)
    col0 = dev_col0 + step * WIDTH
    slab = shared[2 * n : 3 * n]
    slab_hl = stacked_halves(slab)
    groups = cols // parts // 128
    first = step * (WIDTH // (cols // parts))

    def place(k, result):
        for q in range(WIDTH // 128):
            at = (q % groups) * 2 * n + k * n
            out[first + q // groups, at : at + n] = result[:, q * 128 : (q + 1) * 128]

    crossed = col0 <= row0 + rows - 1

    @pl.when(jnp.logical_not(crossed))
    def _():
        for k, matrix in enumerate((sat, ter)):
            place(k, dot_columns(slab_hl, matrix[...]))

    @pl.when(crossed)
    def _():
        r, c = ids(sat.shape, row0, col0)
        for k, matrix in enumerate((sat, ter)):
            place(k, dot_columns(slab_hl, jnp.where(c > r, matrix[...], 0.0)))

    @pl.when(step == 0)
    def _():
        eye = jnp.equal(*ids((n, 128), 0, 0))
        tail = []
        for k in range(2):
            direct = shared[k * n : (k + 1) * n]
            row_part[k] = direct
            diagonal = shared[3 * n + k : 3 * n + k + 1]
            term = jnp.sum(slab * (2.0 * direct - diagonal * slab), axis=1, keepdims=True)
            tail.append(jnp.sum(jnp.where(eye, term, 0.0), axis=0, keepdims=True))
        tail.append(jnp.zeros((6, 128), f32))
        tail = jnp.concatenate(tail, axis=0)
        for part in range(parts):
            out[part, groups * 2 * n : groups * 2 * n + 8] = tail


def column_products(sat, ter, shared, n, parts):
    rows, cols = sat.shape
    chunk = (cols // parts // 128) * 2 * n + 8
    return pl.pallas_call(
        functools.partial(column_kernel, cols, n, parts),
        grid=(cols // WIDTH,),
        in_specs=[
            pl.BlockSpec((rows, WIDTH), lambda j: (0, j)),
            pl.BlockSpec((rows, WIDTH), lambda j: (0, j)),
            pl.BlockSpec(shared.shape, lambda j: (0, 0)),
        ],
        out_specs=[
            pl.BlockSpec((parts, chunk, 128), lambda j: (0, 0, 0)),
            pl.BlockSpec((2, n, rows), lambda j: (0, 0, 0)),
        ],
        out_shape=[
            jax.ShapeDtypeStruct((parts, chunk, 128), f32),
            jax.ShapeDtypeStruct((2, n, rows), f32),
        ],
        name="column_products",
    )(sat, ter, shared)


def sum_kernel(n, arrived, column_part, trace):
    parts, chunk, _ = arrived.shape
    groups = (chunk - 8) // (2 * n)
    total = arrived[0]
    for part in range(1, parts):
        total = total + arrived[part]
    for q in range(groups):
        for k in range(2):
            at = q * 2 * n + k * n
            column_part[k, :, q * 128 : (q + 1) * 128] = total[at : at + n]
    trace[...] = total[groups * 2 * n : groups * 2 * n + 2, :n]


def sum_parts(arrived, n, width):
    return pl.pallas_call(
        functools.partial(sum_kernel, n),
        in_specs=[VMEM],
        out_specs=[VMEM, VMEM],
        out_shape=[
            jax.ShapeDtypeStruct((2, n, width), f32),
            jax.ShapeDtypeStruct((2, n), f32),
        ],
        name="sum_parts",
    )(arrived)


def exchanged_sum(value, axis, bit):
    size = lax.axis_size(axis)
    return value + lax.ppermute(value, axis, [(i, i ^ bit) for i in range(size)])


def shards(matrix_sat, matrix_ter, probes):
    n, cols = probes.shape
    shared = row_products(matrix_sat, matrix_ter, probes)
    for axis in ("blk_2", "blk_0", "blk_1"):
        bit = 1
        while bit < lax.axis_size(axis):
            shared = exchanged_sum(shared, axis, bit)
            bit *= 2
    parts = lax.axis_size(GRP)
    mirrored, row_part = column_products(matrix_sat, matrix_ter, shared, n, parts)
    arrived = lax.all_to_all(mirrored, GRP, split_axis=0, concat_axis=0, tiled=True)
    column_part, trace_terms = sum_parts(arrived, n, cols // parts)
    return row_part, column_part, trace_terms


def solution(mesh):
    split = Mesh(mesh.devices.reshape(2, 8, 2, 2, 4), BLK_GRP)
    in_specs = (P(GRP, BLK), P(GRP, BLK), P(None, BLK))
    out_specs = (P(None, None, GRP), P(None, None, BLK_GRP), P())
    return jax.shard_map(
        shards, mesh=split, in_specs=in_specs, out_specs=out_specs, check_vma=False
    )
```

```python
import functools

import jax
import jax.numpy as jnp
from jax import lax
from jax.experimental import pallas as pl
from jax.experimental.pallas import tpu as pltpu
from jax.sharding import Mesh
from jax.sharding import PartitionSpec as P

BLK = ("blk_0", "blk_1", "blk_2")
GRP = ("grp_0", "grp_1")
BLK_GRP = BLK + GRP
WIDTH = 2048
f32, bf16 = jnp.float32, jnp.bfloat16
VMEM = pl.BlockSpec(memory_space=pltpu.VMEM)


def halves(value):
    high = value.astype(bf16)
    return high, (value - high.astype(f32)).astype(bf16)


def stacked_halves(value):
    return jnp.concatenate(halves(value), axis=0)


def fold(both):
    half = both.shape[0] // 2
    return both[:half] + both[half:]


def dot_rows(probes_hl, high, low):
    dims = (((1,), (1,)), ((), ()))
    return fold(
        lax.dot_general(probes_hl, high, dims, preferred_element_type=f32)
        + lax.dot_general(probes_hl, low, dims, preferred_element_type=f32)
    )


def dot_columns(slab_hl, high, low):
    return fold(
        jnp.dot(slab_hl, high, preferred_element_type=f32)
        + jnp.dot(slab_hl, low, preferred_element_type=f32)
    )


def offsets(rows, cols):
    return lax.axis_index(GRP) * rows, lax.axis_index(BLK) * cols


def ids(shape, row0, col0):
    return (
        row0 + lax.broadcasted_iota(jnp.int32, shape, 0),
        col0 + lax.broadcasted_iota(jnp.int32, shape, 1),
    )


def row_kernel(cols, sat, ter, probes, out, high_out, low_out):
    step = pl.program_id(0)
    rows = sat.shape[0]
    n = probes.shape[0]
    row0, dev_col0 = offsets(rows, cols)
    col0 = dev_col0 + step * WIDTH

    @pl.when(step == 0)
    def _():
        out[...] = jnp.zeros_like(out)

    probes_hl = stacked_halves(probes[...])
    here = pl.ds(pl.multiple_of(step * WIDTH, WIDTH), WIDTH)
    crossed = col0 < row0 + rows

    def products(masked):
        for k, matrix in enumerate((sat, ter)):
            block = matrix[...]
            if masked:
                r, c = ids(block.shape, row0, col0)
                block = jnp.where(c > r, block, 0.0)
            high, low = halves(block)
            high_out[k, :, here] = high
            low_out[k, :, here] = low
            out[k * n : (k + 1) * n] += dot_rows(probes_hl, high, low)

    @pl.when(jnp.logical_not(crossed))
    def _():
        products(False)

    @pl.when(crossed)
    def _():
        products(True)

    @pl.when((row0 >= col0) & (row0 < col0 + WIDTH))
    def _():
        at = pl.ds(pl.multiple_of(row0 - col0, rows), rows)
        slab = probes[:, at]
        out[2 * n : 3 * n] = slab
        r, c = ids((rows, rows), 0, 0)
        for k, matrix in enumerate((sat, ter)):
            diagonal = jnp.sum(jnp.where(r == c, matrix[:, at], 0.0), axis=0, keepdims=True)
            out[3 * n + k : 3 * n + k + 1] = diagonal
            out[k * n : (k + 1) * n] += diagonal * slab


def row_products(sat, ter, probes):
    rows, cols = sat.shape
    n = probes.shape[0]
    return pl.pallas_call(
        functools.partial(row_kernel, cols),
        grid=(cols // WIDTH,),
        in_specs=[
            pl.BlockSpec((rows, WIDTH), lambda j: (0, j)),
            pl.BlockSpec((rows, WIDTH), lambda j: (0, j)),
            pl.BlockSpec((n, WIDTH), lambda j: (0, j)),
        ],
        out_specs=[VMEM] * 3,
        out_shape=[jax.ShapeDtypeStruct((3 * n + 8, rows), f32)]
        + [jax.ShapeDtypeStruct((2, rows, cols), bf16)] * 2,
        compiler_params=pltpu.CompilerParams(vmem_limit_bytes=44 * 2**20),
        name="row_products",
    )(sat, ter, probes)


def column_kernel(cols, n, parts, high, low, held, arrived, out, row_part):
    shared = held[...] + arrived[...]
    slab = shared[2 * n : 3 * n]
    slab_hl = stacked_halves(slab)
    width = cols // parts
    groups = width // 128
    for part in range(parts):
        at = slice(part * width, (part + 1) * width)
        for k in range(2):
            result = dot_columns(slab_hl, high[k, :, at], low[k, :, at])
            for q in range(groups):
                to = q * 2 * n + k * n
                out[part, to : to + n] = result[:, q * 128 : (q + 1) * 128]

    eye = jnp.equal(*ids((n, 128), 0, 0))
    tail = []
    for k in range(2):
        direct = shared[k * n : (k + 1) * n]
        row_part[k] = direct
        diagonal = shared[3 * n + k : 3 * n + k + 1]
        term = jnp.sum(slab * (2.0 * direct - diagonal * slab), axis=1, keepdims=True)
        tail.append(jnp.sum(jnp.where(eye, term, 0.0), axis=0, keepdims=True))
    tail.append(jnp.zeros((6, 128), f32))
    tail = jnp.concatenate(tail, axis=0)
    for part in range(parts):
        out[part, groups * 2 * n : groups * 2 * n + 8] = tail


def column_products(high, low, held, arrived, n, parts):
    _, rows, cols = high.shape
    chunk = (cols // parts // 128) * 2 * n + 8
    return pl.pallas_call(
        functools.partial(column_kernel, cols, n, parts),
        in_specs=[VMEM] * 4,
        out_specs=[VMEM] * 2,
        out_shape=[
            jax.ShapeDtypeStruct((parts, chunk, 128), f32),
            jax.ShapeDtypeStruct((2, n, rows), f32),
        ],
        compiler_params=pltpu.CompilerParams(vmem_limit_bytes=24 * 2**20),
        name="column_products",
    )(high, low, held, arrived)


def sum_kernel(n, arrived, column_part, trace):
    parts, chunk, _ = arrived.shape
    groups = (chunk - 8) // (2 * n)
    total = arrived[0]
    for part in range(1, parts):
        total = total + arrived[part]
    for q in range(groups):
        for k in range(2):
            at = q * 2 * n + k * n
            column_part[k, :, q * 128 : (q + 1) * 128] = total[at : at + n]
    trace[...] = total[groups * 2 * n : groups * 2 * n + 2, :n]


def sum_parts(arrived, n, width):
    return pl.pallas_call(
        functools.partial(sum_kernel, n),
        in_specs=[VMEM],
        out_specs=[VMEM, VMEM],
        out_shape=[
            jax.ShapeDtypeStruct((2, n, width), f32),
            jax.ShapeDtypeStruct((2, n), f32),
        ],
        compiler_params=pltpu.CompilerParams(vmem_limit_bytes=8 * 2**20),
        name="sum_parts",
    )(arrived)


def add_kernel(*refs):
    *terms, out = refs
    sums = [ref[...] for ref in terms]
    while len(sums) > 1:
        sums = [a + b for a, b in zip(sums[::2], sums[1::2], strict=True)]
    out[...] = sums[0]


def added(*terms):
    return pl.pallas_call(
        add_kernel,
        in_specs=[VMEM] * len(terms),
        out_specs=VMEM,
        out_shape=jax.ShapeDtypeStruct(terms[0].shape, f32),
        compiler_params=pltpu.CompilerParams(vmem_limit_bytes=2 * 2**20),
        name="added",
    )(*terms)


def exchanged(value, bits):
    size = lax.axis_size(BLK)
    return lax.ppermute(value, BLK, [(i, i ^ bits) for i in range(size)])


def summed_over_four(value, first, second):
    a, b, c = (exchanged(value, bits) for bits in (first, second, first ^ second))
    return added(value, a, b, c)


def shards(matrix_sat, matrix_ter, probes):
    n, cols = probes.shape
    core, z1, z2, z4, y = 1, 2, 4, 8, 16
    shared, high, low = row_products(matrix_sat, matrix_ter, probes)
    shared = added(shared, exchanged(shared, core))
    shared = summed_over_four(shared, y, z1)
    shared = added(shared, exchanged(shared, z2))
    arrived = exchanged(shared, z4)
    parts = lax.axis_size(GRP)
    mirrored, row_part = column_products(
        high, low, shared, arrived, n, parts
    )
    arrived = lax.all_to_all(mirrored, GRP, split_axis=0, concat_axis=0, tiled=True)
    column_part, trace_terms = sum_parts(arrived, n, cols // parts)
    return row_part, column_part, trace_terms


def solution(mesh):
    split = Mesh(mesh.devices.reshape(2, 8, 2, 2, 4), BLK_GRP)
    in_specs = (P(GRP, BLK), P(GRP, BLK), P(None, BLK))
    out_specs = (P(None, None, GRP), P(None, None, BLK_GRP), P())
    return jax.shard_map(
        shards, mesh=split, in_specs=in_specs, out_specs=out_specs, check_vma=False
    )
```

```python
import functools

import jax
import jax.numpy as jnp
from jax import lax
from jax.experimental import pallas as pl
from jax.experimental.pallas import tpu as pltpu
from jax.sharding import Mesh
from jax.sharding import PartitionSpec as P

BLK = ("blk_0", "blk_1", "blk_2")
GRP = ("grp_0", "grp_1")
BLK_GRP = BLK + GRP
WIDTH = 2048
f32, bf16 = jnp.float32, jnp.bfloat16
VMEM = pl.BlockSpec(memory_space=pltpu.VMEM)


def in_hbm(value):
    return pltpu.with_memory_space_constraint(value, pltpu.HBM)


def halves(value):
    high = value.astype(bf16)
    return high, (value - high.astype(f32)).astype(bf16)


def stacked_halves(value):
    return jnp.concatenate(halves(value), axis=0)


def fold(both):
    half = both.shape[0] // 2
    return both[:half] + both[half:]


def dot_rows(probes_hl, high, low):
    dims = (((1,), (1,)), ((), ()))
    return fold(
        lax.dot_general(probes_hl, high, dims, preferred_element_type=f32)
        + lax.dot_general(low, probes_hl, dims, preferred_element_type=f32).T
    )


def dot_columns(slab_hl, high, low):
    return fold(
        jnp.dot(slab_hl, high, preferred_element_type=f32)
        + jnp.dot(slab_hl, low, preferred_element_type=f32)
    )


def offsets(rows, cols):
    return lax.axis_index(GRP) * rows, lax.axis_index(BLK) * cols


def ids(shape, row0, col0):
    return (
        row0 + lax.broadcasted_iota(jnp.int32, shape, 0),
        col0 + lax.broadcasted_iota(jnp.int32, shape, 1),
    )


def put(ref, start, stride, value):
    size, lanes = value.shape
    for q in range(lanes // 128):
        ref[start + q * stride : start + q * stride + size] = value[:, q * 128 : (q + 1) * 128]


def take(ref, start, size, stride, lanes):
    return jnp.concatenate(
        [ref[start + q * stride : start + q * stride + size] for q in range(lanes // 128)], axis=1
    )


def row_kernel(cols, sat, ter, probes, out, high_out, low_out):
    step = pl.program_id(0)
    rows = sat.shape[0]
    n = probes.shape[0]
    row0, dev_col0 = offsets(rows, cols)
    col0 = dev_col0 + step * WIDTH

    @pl.when(step == 0)
    def _():
        out[...] = jnp.zeros_like(out)

    probes_hl = stacked_halves(probes[...])
    here = pl.ds(pl.multiple_of(step * WIDTH, WIDTH), WIDTH)
    crossed = col0 < row0 + rows

    def products(masked):
        for k, matrix in enumerate((sat, ter)):
            block = matrix[...]
            if masked:
                r, c = ids(block.shape, row0, col0)
                block = jnp.where(c > r, block, 0.0)
            high, low = halves(block)
            high_out[k, :, here] = high
            low_out[k, :, here] = low
            sums = take(out, k * n, n, 2 * n, rows) + dot_rows(probes_hl, high, low)
            put(out, k * n, 2 * n, sums)

    @pl.when(jnp.logical_not(crossed))
    def _():
        products(False)

    @pl.when(crossed)
    def _():
        products(True)

    @pl.when((row0 >= col0) & (row0 < col0 + WIDTH))
    def _():
        at = pl.ds(pl.multiple_of(row0 - col0, rows), rows)
        slab = probes[:, at]
        put(out, 4 * n, n, slab)
        r, c = ids((rows, rows), 0, 0)
        for k, matrix in enumerate((sat, ter)):
            diagonal = jnp.sum(jnp.where(r == c, matrix[:, at], 0.0), axis=0, keepdims=True)
            put(out, 6 * n + k, 2, diagonal)
            put(out, k * n, 2 * n, take(out, k * n, n, 2 * n, rows) + diagonal * slab)


def row_products(sat, ter, probes):
    rows, cols = sat.shape
    n = probes.shape[0]
    return pl.pallas_call(
        functools.partial(row_kernel, cols),
        grid=(cols // WIDTH,),
        in_specs=[
            pl.BlockSpec((rows, WIDTH), lambda j: (0, j)),
            pl.BlockSpec((rows, WIDTH), lambda j: (0, j)),
            pl.BlockSpec((n, WIDTH), lambda j: (0, j)),
        ],
        out_specs=[VMEM] * 3,
        out_shape=[jax.ShapeDtypeStruct((3 * n * (rows // 128) + 8, 128), f32)]
        + [jax.ShapeDtypeStruct((2, rows, cols), bf16)] * 2,
        compiler_params=pltpu.CompilerParams(vmem_limit_bytes=44 * 2**20),
        name="row_products",
    )(in_hbm(sat), in_hbm(ter), in_hbm(probes))


def column_kernel(cols, n, parts, high, low, held, arrived, out, row_part):
    shared = held[...] + arrived[...]
    rows = row_part.shape[2]
    slab = take(shared, 4 * n, n, n, rows)
    slab_hl = stacked_halves(slab)
    width = cols // parts
    groups = width // 128
    for part in range(parts):
        at = slice(part * width, (part + 1) * width)
        for k in range(2):
            result = dot_columns(slab_hl, high[k, :, at], low[k, :, at])
            for q in range(groups):
                to = q * 2 * n + k * n
                out[part, to : to + n] = result[:, q * 128 : (q + 1) * 128]

    eye = jnp.equal(*ids((n, 128), 0, 0))
    tail = []
    for k in range(2):
        direct = take(shared, k * n, n, 2 * n, rows)
        row_part[k] = direct
        diagonal = take(shared, 6 * n + k, 1, 2, rows)
        term = jnp.sum(slab * (2.0 * direct - diagonal * slab), axis=1, keepdims=True)
        tail.append(jnp.sum(jnp.where(eye, term, 0.0), axis=0, keepdims=True))
    tail.append(jnp.zeros((6, 128), f32))
    tail = jnp.concatenate(tail, axis=0)
    for part in range(parts):
        out[part, groups * 2 * n : groups * 2 * n + 8] = tail


def column_products(high, low, held, arrived, n, parts):
    _, rows, cols = high.shape
    chunk = (cols // parts // 128) * 2 * n + 8
    return pl.pallas_call(
        functools.partial(column_kernel, cols, n, parts),
        in_specs=[VMEM] * 4,
        out_specs=[VMEM] * 2,
        out_shape=[
            jax.ShapeDtypeStruct((parts, chunk, 128), f32),
            jax.ShapeDtypeStruct((2, n, rows), f32),
        ],
        compiler_params=pltpu.CompilerParams(vmem_limit_bytes=24 * 2**20),
        name="column_products",
    )(high, low, held, arrived)


def sum_kernel(n, arrived, column_part, trace):
    parts, chunk, _ = arrived.shape
    groups = (chunk - 8) // (2 * n)
    total = arrived[0]
    for part in range(1, parts):
        total = total + arrived[part]
    for q in range(groups):
        for k in range(2):
            at = q * 2 * n + k * n
            column_part[k, :, q * 128 : (q + 1) * 128] = total[at : at + n]
    trace[...] = total[groups * 2 * n : groups * 2 * n + 2, :n]


def sum_parts(arrived, n, width):
    return pl.pallas_call(
        functools.partial(sum_kernel, n),
        in_specs=[VMEM],
        out_specs=[VMEM, VMEM],
        out_shape=[
            jax.ShapeDtypeStruct((2, n, width), f32),
            jax.ShapeDtypeStruct((2, n), f32),
        ],
        compiler_params=pltpu.CompilerParams(vmem_limit_bytes=8 * 2**20),
        name="sum_parts",
    )(arrived)


def add_kernel(*refs):
    *terms, out = refs
    sums = [ref[...] for ref in terms]
    while len(sums) > 1:
        sums = [a + b for a, b in zip(sums[::2], sums[1::2], strict=True)]
    out[...] = sums[0]


def added(*terms):
    return pl.pallas_call(
        add_kernel,
        in_specs=[VMEM] * len(terms),
        out_specs=VMEM,
        out_shape=jax.ShapeDtypeStruct(terms[0].shape, f32),
        compiler_params=pltpu.CompilerParams(vmem_limit_bytes=2 * 2**20),
        name="added",
    )(*terms)


def exchanged(value, bits):
    size = lax.axis_size(BLK)
    return lax.ppermute(value, BLK, [(i, i ^ bits) for i in range(size)])


def summed_over_four(value, first, second):
    a, b, c = (exchanged(value, bits) for bits in (first, second, first ^ second))
    return added(value, a, b, c)


def shards(matrix_sat, matrix_ter, probes):
    n, cols = probes.shape
    core, z1, z2, z4, y = 1, 2, 4, 8, 16
    shared, high, low = row_products(matrix_sat, matrix_ter, probes)
    shared = added(shared, exchanged(shared, core))
    shared = summed_over_four(shared, y, z1)
    shared = added(shared, exchanged(shared, z2))
    arrived = exchanged(shared, z4)
    parts = lax.axis_size(GRP)
    mirrored, row_part = column_products(
        high, low, shared, arrived, n, parts
    )
    arrived = lax.all_to_all(mirrored, GRP, split_axis=0, concat_axis=0, tiled=True)
    column_part, trace_terms = sum_parts(arrived, n, cols // parts)
    return row_part, column_part, trace_terms


def solution(mesh):
    split = Mesh(mesh.devices.reshape(2, 8, 2, 2, 4), BLK_GRP)
    in_specs = (P(GRP, BLK), P(GRP, BLK), P(None, BLK))
    out_specs = (P(None, None, GRP), P(None, None, BLK_GRP), P())
    return jax.shard_map(
        shards, mesh=split, in_specs=in_specs, out_specs=out_specs, check_vma=False
    )
```

```python
import functools

import jax
import jax.numpy as jnp
from jax import lax
from jax.experimental import pallas as pl
from jax.experimental.pallas import tpu as pltpu
from jax.sharding import Mesh
from jax.sharding import PartitionSpec as P

BLK = ("blk_0", "blk_1", "blk_2")
GRP = ("grp_0", "grp_1")
BLK_GRP = BLK + GRP
WIDTH = 2048
f32, bf16 = jnp.float32, jnp.bfloat16
VMEM = pl.BlockSpec(memory_space=pltpu.VMEM)


def in_hbm(value):
    return pltpu.with_memory_space_constraint(value, pltpu.HBM)


def halves(value):
    high = value.astype(bf16)
    return high, (value - high.astype(f32)).astype(bf16)


def stacked_halves(value):
    return jnp.concatenate(halves(value), axis=0)


def fold(both):
    half = both.shape[0] // 2
    return both[:half] + both[half:]


def dot_rows(probes_hl, high, low):
    dims = (((1,), (1,)), ((), ()))
    return fold(
        lax.dot_general(probes_hl, high, dims, preferred_element_type=f32)
        + lax.dot_general(low, probes_hl, dims, preferred_element_type=f32).T
    )


def dot_columns(slab_hl, high, low):
    return fold(
        jnp.dot(slab_hl, high, preferred_element_type=f32)
        + jnp.dot(slab_hl, low, preferred_element_type=f32)
    )


def offsets(rows, cols):
    return lax.axis_index(GRP) * rows, lax.axis_index(BLK) * cols


def ids(shape, row0, col0):
    return (
        row0 + lax.broadcasted_iota(jnp.int32, shape, 0),
        col0 + lax.broadcasted_iota(jnp.int32, shape, 1),
    )


def put(ref, start, stride, value):
    size, lanes = value.shape
    for q in range(lanes // 128):
        ref[start + q * stride : start + q * stride + size] = value[:, q * 128 : (q + 1) * 128]


def take(ref, start, size, stride, lanes):
    return jnp.concatenate(
        [ref[start + q * stride : start + q * stride + size] for q in range(lanes // 128)], axis=1
    )


def row_kernel(cols, sat, ter, probes, out, high_out, low_out):
    step = pl.program_id(0)
    rows = sat.shape[0]
    n = probes.shape[0]
    row0, dev_col0 = offsets(rows, cols)
    col0 = dev_col0 + step * WIDTH

    @pl.when(step == 0)
    def _():
        out[...] = jnp.zeros_like(out)

    probes_hl = stacked_halves(probes[...])
    here = pl.ds(pl.multiple_of(step * WIDTH, WIDTH), WIDTH)
    crossed = col0 < row0 + rows

    def products(masked):
        for k, matrix in enumerate((sat, ter)):
            block = matrix[...]
            if masked:
                r, c = ids(block.shape, row0, col0)
                block = jnp.where(c > r, block, 0.0)
            high, low = halves(block)
            high_out[k, :, here] = high
            low_out[k, :, here] = low
            sums = take(out, k * n, n, 2 * n, rows) + dot_rows(probes_hl, high, low)
            put(out, k * n, 2 * n, sums)

    @pl.when(jnp.logical_not(crossed))
    def _():
        products(False)

    @pl.when(crossed)
    def _():
        products(True)

    @pl.when((row0 >= col0) & (row0 < col0 + WIDTH))
    def _():
        at = pl.ds(pl.multiple_of(row0 - col0, rows), rows)
        slab = probes[:, at]
        put(out, 4 * n, n, slab)
        r, c = ids((rows, rows), 0, 0)
        for k, matrix in enumerate((sat, ter)):
            diagonal = jnp.sum(jnp.where(r == c, matrix[:, at], 0.0), axis=0, keepdims=True)
            put(out, 6 * n + k, 2, diagonal)
            put(out, k * n, 2 * n, take(out, k * n, n, 2 * n, rows) + diagonal * slab)


def row_products(sat, ter, probes):
    rows, cols = sat.shape
    n = probes.shape[0]
    return pl.pallas_call(
        functools.partial(row_kernel, cols),
        grid=(cols // WIDTH,),
        in_specs=[
            pl.BlockSpec((rows, WIDTH), lambda j: (0, j)),
            pl.BlockSpec((rows, WIDTH), lambda j: (0, j)),
            pl.BlockSpec((n, WIDTH), lambda j: (0, j)),
        ],
        out_specs=[VMEM] * 3,
        out_shape=[jax.ShapeDtypeStruct((3 * n * (rows // 128) + 8, 128), f32)]
        + [jax.ShapeDtypeStruct((2, rows, cols), bf16)] * 2,
        compiler_params=pltpu.CompilerParams(vmem_limit_bytes=44 * 2**20),
        name="row_products",
    )(in_hbm(sat), in_hbm(ter), in_hbm(probes))


def column_kernel(cols, n, parts, high, low, held, arrived, out, row_part):
    shared = held[...] + arrived[...]
    rows = row_part.shape[2]
    slab = take(shared, 4 * n, n, n, rows)
    slab_hl = stacked_halves(slab)
    width = cols // parts
    groups = width // 128
    for part in range(parts):
        at = slice(part * width, (part + 1) * width)
        for k in range(2):
            result = dot_columns(slab_hl, high[k, :, at], low[k, :, at])
            for q in range(groups):
                to = q * 2 * n + k * n
                out[part, to : to + n] = result[:, q * 128 : (q + 1) * 128]

    eye = jnp.equal(*ids((n, 128), 0, 0))
    tail = []
    for k in range(2):
        direct = take(shared, k * n, n, 2 * n, rows)
        row_part[k] = direct
        diagonal = take(shared, 6 * n + k, 1, 2, rows)
        term = jnp.sum(slab * (2.0 * direct - diagonal * slab), axis=1, keepdims=True)
        tail.append(jnp.sum(jnp.where(eye, term, 0.0), axis=0, keepdims=True))
    tail.append(jnp.zeros((6, 128), f32))
    tail = jnp.concatenate(tail, axis=0)
    for part in range(parts):
        out[part, groups * 2 * n : groups * 2 * n + 8] = tail


def column_products(high, low, held, arrived, n, parts):
    _, rows, cols = high.shape
    chunk = (cols // parts // 128) * 2 * n + 8
    return pl.pallas_call(
        functools.partial(column_kernel, cols, n, parts),
        in_specs=[VMEM] * 4,
        out_specs=[VMEM] * 2,
        out_shape=[
            jax.ShapeDtypeStruct((parts, chunk, 128), f32),
            jax.ShapeDtypeStruct((2, n, rows), f32),
        ],
        compiler_params=pltpu.CompilerParams(vmem_limit_bytes=24 * 2**20),
        name="column_products",
    )(high, low, held, arrived)


def sum_kernel(n, arrived, column_part, trace):
    parts, chunk, _ = arrived.shape
    groups = (chunk - 8) // (2 * n)
    total = arrived[0]
    for part in range(1, parts):
        total = total + arrived[part]
    for q in range(groups):
        for k in range(2):
            at = q * 2 * n + k * n
            column_part[k, :, q * 128 : (q + 1) * 128] = total[at : at + n]
    trace[...] = total[groups * 2 * n : groups * 2 * n + 2, :n]


def sum_parts(arrived, n, width):
    return pl.pallas_call(
        functools.partial(sum_kernel, n),
        in_specs=[VMEM],
        out_specs=[VMEM, VMEM],
        out_shape=[
            jax.ShapeDtypeStruct((2, n, width), f32),
            jax.ShapeDtypeStruct((2, n), f32),
        ],
        compiler_params=pltpu.CompilerParams(vmem_limit_bytes=8 * 2**20),
        name="sum_parts",
    )(arrived)


def add_kernel(*refs):
    *terms, out = refs
    sums = [ref[...] for ref in terms]
    while len(sums) > 1:
        sums = [a + b for a, b in zip(sums[::2], sums[1::2], strict=True)]
    out[...] = sums[0]


def added(*terms):
    return pl.pallas_call(
        add_kernel,
        in_specs=[VMEM] * len(terms),
        out_specs=VMEM,
        out_shape=jax.ShapeDtypeStruct(terms[0].shape, f32),
        compiler_params=pltpu.CompilerParams(vmem_limit_bytes=2 * 2**20),
        name="added",
    )(*terms)


def exchanged(value, bits):
    size = lax.axis_size(BLK)
    return lax.ppermute(value, BLK, [(i, i ^ bits) for i in range(size)])


def summed_over_four(value, first, second):
    a, b, c = (exchanged(value, bits) for bits in (first, second, first ^ second))
    return added(value, a, b, c)


def shards(matrix_sat, matrix_ter, probes):
    n, cols = probes.shape
    core, z1, z2, z4, y = 1, 2, 4, 8, 16
    shared, high, low = row_products(matrix_sat, matrix_ter, probes)
    shared = added(shared, exchanged(shared, core))
    shared = summed_over_four(shared, y, z1)
    shared = added(shared, exchanged(shared, z4))
    arrived = exchanged(shared, z2)
    parts = lax.axis_size(GRP)
    mirrored, row_part = column_products(
        high, low, shared, arrived, n, parts
    )
    arrived = lax.all_to_all(mirrored, GRP, split_axis=0, concat_axis=0, tiled=True)
    column_part, trace_terms = sum_parts(arrived, n, cols // parts)
    return row_part, column_part, trace_terms


def solution(mesh):
    split = Mesh(mesh.devices.reshape(2, 8, 2, 2, 4), BLK_GRP)
    in_specs = (P(GRP, BLK), P(GRP, BLK), P(None, BLK))
    out_specs = (P(None, None, GRP), P(None, None, BLK_GRP), P())
    return jax.shard_map(
        shards, mesh=split, in_specs=in_specs, out_specs=out_specs, check_vma=False
    )
```
